32 devices in a mesh: fsdp: 4 (over z), seq: 8 (over y, x, core).
Axes of the slice: x: 2, y: 2, z: 4, core: 2. Of those that a mesh axis runs over, the one named last changes fastest.
Arguments:
- layer_input: bfloat16 [8, 512, 2048], P('fsdp', 'seq'), may hold values from -6 to 6
- positions: int32 [8, 512], P('fsdp'), may hold values from 0 to 511, each once within a row
- q_weight: bfloat16 [2048, 2048], P(('fsdp', 'seq')), may hold values from -0.125 to 0.125
- k_weight: bfloat16 [2048, 512], P(('fsdp', 'seq')), may hold values from -0.125 to 0.125
- v_weight: bfloat16 [2048, 512], P(('fsdp', 'seq')), may hold values from -0.125 to 0.125
- out_weight: bfloat16 [2048, 2048], P(('fsdp', 'seq')), may hold values from -1.5 to 1.5
- attn_gain: bfloat16 [2048], P(('fsdp', 'seq')), may hold values from 0.5 to 1.5
- gate_weight: bfloat16 [2048, 8192], P(('fsdp', 'seq')), may hold values from -0.125 to 0.125
- up_weight: bfloat16 [2048, 8192], P(('fsdp', 'seq')), may hold values from -0.125 to 0.125
- down_weight: bfloat16 [8192, 2048], P(('fsdp', 'seq')), may hold values from -0.0625 to 0.0625
- mlp_gain: bfloat16 [2048], P(('fsdp', 'seq')), may hold values from 0.5 to 1.5
- cotangent: bfloat16 [8, 512, 2048], P('fsdp', 'seq'), may hold values from -6 to 6
Outputs:
- output: bfloat16 [8, 512, 2048], P('fsdp', 'seq')
- input_grad: float32 [8, 512, 2048], P('fsdp', 'seq')
- q_grad: float32 [2048, 2048], P(('fsdp', 'seq'))
- k_grad: float32 [2048, 512], P(('fsdp', 'seq'))
- v_grad: float32 [2048, 512], P(('fsdp', 'seq'))
- out_grad: float32 [2048, 2048], P(('fsdp', 'seq'))
- attn_gain_grad: float32 [2048], P(('fsdp', 'seq'))
- gate_grad: float32 [2048, 8192], P(('fsdp', 'seq'))
- up_grad: float32 [2048, 8192], P(('fsdp', 'seq'))
- down_grad: float32 [8192, 2048], P(('fsdp', 'seq'))
- mlp_gain_grad: float32 [2048], P(('fsdp', 'seq'))
The draws below stay inside these ranges and needn't reach their ends.
Inputs may be any that keep to these rules, and one draw needn't show every extreme that they name: Each row of positions holds every position 0 to 511 once.
All inputs are finite; a program needn't handle non-finite values.
Results may differ from the reference program's by a relative error of at most 0.014.
Values may be sent and summed in bfloat16 or wider, within the bound.
No kernel may reach another device: no remote copies, remote signals or barrier semaphores. Data moves between devices by JAX's collectives and lax.ppermute only.
A program may use at most 256 MiB of HBM per device.

```python
import math
import jax
import jax.numpy as jnp
from jax import lax

D = 2048
H = 32
KV = 8
HD = 64
FF = 8192
LEN = 512
SEQS = 8


def block_levels(rng, extent, shards, least, top_value):
    def one(axis_at, blocks):
        heights = jax.random.uniform(jax.random.fold_in(jax.random.fold_in(rng, 6), axis_at), (blocks,), jnp.float32, least / len(shards), top_value / len(shards))
        return jnp.repeat(jnp.exp(heights), extent[axis_at] // blocks).reshape((-1,) + (1,) * (len(extent) - axis_at - 1))

    level = one(*shards[0])
    for cut in shards[1:]:
        level = level * one(*cut)
    return level


def centred(own_key, extent, spread, reach, cuts=(), dtype=jnp.bfloat16):
    entries = spread * jax.random.normal(own_key, extent, jnp.float32)
    if cuts:
        entries = entries * block_levels(own_key, extent, cuts, -0.22, 0.18)
    return jnp.clip(entries, -reach, reach).astype(dtype)


def setup_inputs(seed: int = 0) -> dict:
    key_of = jax.random.split(jax.random.key(seed), 13)
    return {
        "layer_input": centred(key_of[0], (SEQS, LEN, D), 1.0, 6.0, ((0, 4), (1, 8))),
        "positions": jax.vmap(lambda own: jax.random.permutation(own, LEN))(jax.random.split(key_of[1], SEQS)).reshape((SEQS, LEN)).astype(jnp.int32),
        "q_weight": centred(key_of[2], (D, H * HD), D ** -0.5, 0.125, ((0, 32),)),
        "k_weight": centred(key_of[3], (D, KV * HD), D ** -0.5, 0.125, ((0, 32),)),
        "v_weight": centred(key_of[4], (D, KV * HD), D ** -0.5, 0.125, ((0, 32),)),
        "out_weight": centred(key_of[5], (H * HD, D), (H * HD // 128) ** -0.5, 1.5, ((0, 32),)),
        "attn_gain": jnp.clip(1.0 + 0.1 * jax.random.normal(key_of[6], (D,), jnp.float32), 0.5, 1.5).astype(jnp.bfloat16),
        "gate_weight": centred(key_of[7], (D, FF), D ** -0.5, 0.125, ((0, 32),)),
        "up_weight": centred(key_of[8], (D, FF), D ** -0.5, 0.125, ((0, 32),)),
        "down_weight": centred(key_of[9], (FF, D), FF ** -0.5, 0.0625, ((0, 32),)),
        "mlp_gain": jnp.clip(1.0 + 0.1 * jax.random.normal(key_of[10], (D,), jnp.float32), 0.5, 1.5).astype(jnp.bfloat16),
        "cotangent": centred(key_of[11], (SEQS, LEN, D), 1.0, 6.0, ((0, 4), (1, 8))),
    }


EPS = 1e-05
THETA = 500000.0
NEG = -1e+30

def rotate(vec, pos, sign):
    half = vec.shape[-1] // 2
    freq = THETA ** (-(jnp.arange(half).astype(jnp.float32) * 2.0 / vec.shape[-1]))
    angle = pos.astype(jnp.float32)[:, None] * freq[None, :]
    cosine = jnp.cos(angle)[:, None, :]
    sine = sign * jnp.sin(angle)[:, None, :]
    first = vec[..., :half]
    second = vec[..., half:]
    return jnp.concatenate([first * cosine - second * sine, second * cosine + first * sine], axis=-1)

def norm_fwd(stream, gain):
    rinv = lax.rsqrt(lax.optimization_barrier(jnp.mean(stream * stream, axis=-1, keepdims=True)) + EPS)
    return (rinv, (stream * rinv * gain.astype(jnp.float32)).astype(jnp.bfloat16))

def norm_bwd(stream, rinv, gain, d_normed):
    scaled = d_normed * gain.astype(jnp.float32)
    d_stream = rinv * scaled - stream * (rinv * rinv * rinv) * lax.optimization_barrier(jnp.mean(scaled * stream, axis=-1, keepdims=True))
    return (d_stream, lax.optimization_barrier(jnp.sum(d_normed * stream * rinv, axis=0)))

def attend(query, key, value, qpos, kpos):
    scale = 1.0 / math.sqrt(HD)
    allowed = kpos[None, :] <= qpos[:, None]
    score = jnp.where(allowed, jnp.dot(query, key.T, preferred_element_type=jnp.float32) * scale, NEG)
    top = lax.optimization_barrier(jnp.max(score, axis=-1, keepdims=True))
    expo = jnp.where(allowed, jnp.exp(score - top), 0.0)
    total = lax.optimization_barrier(jnp.sum(expo, axis=-1, keepdims=True))
    mixed = jnp.dot(expo.astype(jnp.bfloat16), value, preferred_element_type=jnp.float32) / total
    return (mixed.astype(jnp.bfloat16), top[:, 0] + jnp.log(total[:, 0]))

def attend_back(query, key, value, outv, dout, lse, qpos, kpos):
    scale = 1.0 / math.sqrt(HD)
    allowed = kpos[None, :] <= qpos[:, None]
    score = jnp.dot(query, key.T, preferred_element_type=jnp.float32) * scale
    probs = jnp.where(allowed, jnp.exp(score - lse[:, None]), 0.0)
    value_grad = jnp.dot(probs.astype(jnp.bfloat16).T, dout, preferred_element_type=jnp.float32)
    dprob = jnp.dot(dout, value.T, preferred_element_type=jnp.float32)
    delta = lax.optimization_barrier(jnp.sum(dout.astype(jnp.float32) * outv.astype(jnp.float32), axis=-1, keepdims=True))
    dscore = (probs * (dprob - delta) * scale).astype(jnp.bfloat16)
    query_grad = jnp.dot(dscore, key, preferred_element_type=jnp.float32)
    key_grad = jnp.dot(dscore.T, query, preferred_element_type=jnp.float32)
    return (query_grad, key_grad, value_grad)

def one_sequence(stream_in, pos, cot, weights):
    q_weight, k_weight, v_weight, out_weight, attn_gain, gate_weight, up_weight, down_weight, mlp_gain = weights
    group = H // KV
    length = stream_in.shape[0]
    f32 = jnp.float32
    bf16 = jnp.bfloat16
    stream = stream_in.astype(f32)
    rinv_one, normed_one = norm_fwd(stream, attn_gain)
    query = rotate(jnp.dot(normed_one, q_weight, preferred_element_type=f32).reshape(length, H, HD), pos, 1.0).astype(bf16)
    key = rotate(jnp.dot(normed_one, k_weight, preferred_element_type=f32).reshape(length, KV, HD), pos, 1.0).astype(bf16)
    value = jnp.dot(normed_one, v_weight, preferred_element_type=f32).astype(bf16).reshape(length, KV, HD)
    query_groups = query.reshape(length, KV, group, HD).transpose(1, 2, 0, 3).reshape(KV, group * length, HD)
    key_groups = key.transpose(1, 0, 2)
    value_groups = value.transpose(1, 0, 2)
    query_pos = jnp.tile(pos, group)
    out_groups, lse = lax.map(lambda item: attend(item[0], item[1], item[2], query_pos, pos), (query_groups, key_groups, value_groups))
    attn_out = out_groups.reshape(KV, group, length, HD).transpose(2, 0, 1, 3).reshape(length, H * HD)
    mixed = stream + jnp.dot(attn_out, out_weight, preferred_element_type=f32)
    rinv_two, normed_two = norm_fwd(mixed, mlp_gain)
    gate_pre = jnp.dot(normed_two, gate_weight, preferred_element_type=f32)
    up_pre = jnp.dot(normed_two, up_weight, preferred_element_type=f32)
    sigm = jax.nn.sigmoid(gate_pre)
    silu_val = gate_pre * sigm
    hidden = (silu_val * up_pre).astype(bf16)
    output = (mixed + jnp.dot(hidden, down_weight, preferred_element_type=f32)).astype(bf16)
    grad_f = cot.astype(f32)
    d_hidden = jnp.dot(cot, down_weight.T, preferred_element_type=f32)
    down_grad = jnp.dot(hidden.T, cot, preferred_element_type=f32)
    grad_gate = (d_hidden * up_pre * sigm * (1.0 + gate_pre * (1.0 - sigm))).astype(bf16)
    grad_up = (d_hidden * silu_val).astype(bf16)
    gate_grad = jnp.dot(normed_two.T, grad_gate, preferred_element_type=f32)
    up_grad = jnp.dot(normed_two.T, grad_up, preferred_element_type=f32)
    d_norm_two = jnp.dot(grad_gate, gate_weight.T, preferred_element_type=f32) + jnp.dot(grad_up, up_weight.T, preferred_element_type=f32)
    d_two, mlp_gain_grad = norm_bwd(mixed, rinv_two, mlp_gain, d_norm_two)
    d_mixed = grad_f + d_two
    d_mixed_b = d_mixed.astype(bf16)
    out_grad = jnp.dot(attn_out.T, d_mixed_b, preferred_element_type=f32)
    d_attn = jnp.dot(d_mixed_b, out_weight.T, preferred_element_type=f32).astype(bf16)
    d_groups = d_attn.reshape(length, KV, group, HD).transpose(1, 2, 0, 3).reshape(KV, group * length, HD)
    dq_groups, dk_groups, dv_groups = lax.map(lambda item: attend_back(item[0], item[1], item[2], item[3], item[4], item[5], query_pos, pos), (query_groups, key_groups, value_groups, out_groups, d_groups, lse))
    dq_rows = dq_groups.reshape(KV, group, length, HD).transpose(2, 0, 1, 3).reshape(length, H, HD)
    query_grad = rotate(dq_rows, pos, -1.0).reshape(length, H * HD).astype(bf16)
    key_grad = rotate(dk_groups.transpose(1, 0, 2), pos, -1.0).reshape(length, KV * HD).astype(bf16)
    value_grad = dv_groups.transpose(1, 0, 2).reshape(length, KV * HD).astype(bf16)
    q_grad = jnp.dot(normed_one.T, query_grad, preferred_element_type=f32)
    k_grad = jnp.dot(normed_one.T, key_grad, preferred_element_type=f32)
    v_grad = jnp.dot(normed_one.T, value_grad, preferred_element_type=f32)
    d_norm_one = jnp.dot(query_grad, q_weight.T, preferred_element_type=f32) + jnp.dot(key_grad, k_weight.T, preferred_element_type=f32) + jnp.dot(value_grad, v_weight.T, preferred_element_type=f32)
    d_one, attn_gain_grad = norm_bwd(stream, rinv_one, attn_gain, d_norm_one)
    input_grad = d_mixed + d_one
    grads = (q_grad, k_grad, v_grad, out_grad, attn_gain_grad, gate_grad, up_grad, down_grad, mlp_gain_grad)
    return (output, input_grad, grads)

def reference(layer_input, positions, q_weight, k_weight, v_weight, out_weight, attn_gain, gate_weight, up_weight, down_weight, mlp_gain, cotangent):
    weights = (q_weight, k_weight, v_weight, out_weight, attn_gain, gate_weight, up_weight, down_weight, mlp_gain)
    zeros = tuple((jnp.zeros(w.shape, jnp.float32) for w in weights))

    def step(carry, item):
        stream_in, pos, cot = item
        output, input_grad, grads = one_sequence(stream_in, pos, cot, weights)
        return (tuple((c + g for c, g in zip(carry, grads))), (output, input_grad))
    grads, (outputs, input_grads) = lax.scan(step, zeros, (layer_input, positions, cotangent))
    return (outputs, input_grads, grads[0], grads[1], grads[2], grads[3], grads[4], grads[5], grads[6], grads[7], grads[8])
```

```python
import functools
import math

import jax
import jax.numpy as jnp
from jax import lax
from jax.experimental import pallas as pl
from jax.experimental.pallas import tpu as pltpu
from jax.sharding import Mesh
from jax.sharding import PartitionSpec as P

H = 32
KV = 8
HD = 64

EPS = 1e-05
THETA = 500000.0
NEG = -1e30


f32 = jnp.float32
bf16 = jnp.bfloat16


def xor_perm(x, axis, index):
    n = x.shape[axis]
    bit = 1
    while bit < n:
        shape = x.shape[:axis] + (n // (2 * bit), 2, bit) + x.shape[axis + 1 :]
        y = x.reshape(shape)
        flipped = lax.rev(y, (axis + 1,)).reshape(x.shape)
        x = jnp.where((index // bit) % 2 == 1, flipped, x)
        bit *= 2
    return x


def swap_core(x):
    return lax.ppermute(x, "c", [(0, 1), (1, 0)])


def to_chip(x, k):
    n = lax.axis_size("p")
    return lax.ppermute(x, "p", [(i, i ^ k) for i in range(n)])


def chip_gather(x):
    n = lax.axis_size("p")
    return jnp.concatenate([x] + [to_chip(x, k) for k in range(1, n)], axis=0)


def chip_gather_at(x, chip):
    n = lax.axis_size("p")
    rows = x.shape[0]
    full = jnp.zeros((n * rows,) + x.shape[1:], x.dtype)
    for k in range(n):
        piece = to_chip(x, k) if k else x
        full = lax.dynamic_update_slice_in_dim(full, piece, (chip ^ k) * rows, 0)
    return full


def chip_scatter(x, chip=None):
    n = lax.axis_size("p")
    blk = x.shape[0] // n
    if chip is None:
        parts = [x[k * blk : (k + 1) * blk] for k in range(n)]
    else:
        parts = [lax.dynamic_slice_in_dim(x, (chip ^ k) * blk, blk, 0) for k in range(n)]
    total = parts[0].astype(f32)
    for k in range(1, n):
        total = total + to_chip(parts[k].astype(bf16), k).astype(f32)
    return total


def plane_gather(x):
    n = lax.axis_size("p")
    same = jnp.concatenate([x] + [to_chip(x, k) for k in range(1, n)], axis=1)
    return jnp.concatenate([same, swap_core(same)], axis=1)


def plane_scatter(x):
    n = lax.axis_size("p")
    half = x.shape[1] // 2
    tok = half // n
    recv = swap_core(x[:, half:].astype(bf16))
    both = x[:, :half].astype(f32) + recv.astype(f32)
    total = both[:, :tok]
    for k in range(1, n):
        part = both[:, k * tok : (k + 1) * tok].astype(bf16)
        total = total + to_chip(part, k).astype(f32)
    return total


def rope(z, cosine, sine, lane):
    partner = jnp.where(lane % 64 < 32, jnp.roll(z, -32, axis=1), jnp.roll(z, 32, axis=1))
    return z * cosine + partner * sine


def fwd_kernel(heads, q_ref, kv_ref, cosq_ref, sinq_ref, cosk_ref, sink_ref, qpos_ref, kpos_ref,
               qr_ref, k2_ref, v2_ref, o_ref, lse_ref):
    scale = 1.0 / math.sqrt(HD)
    blk = q_ref.shape[0]

    @pl.when(pl.program_id(1) == 0)
    def _():
        kv = kv_ref[...]
        lane = lax.broadcasted_iota(jnp.int32, kv.shape, 1)
        rot = rope(kv, cosk_ref[...], sink_ref[...], lane)
        k2_ref[...] = jnp.where(lane < 64, rot, pltpu.roll(rot, 64, 1)).astype(bf16)
        v2_ref[...] = jnp.where(lane < 64, pltpu.roll(kv, 64, 1), kv).astype(bf16)

    lane = lax.broadcasted_iota(jnp.int32, (blk, 128), 1)
    allowed = kpos_ref[0] <= qpos_ref[...]
    k2 = k2_ref[...]
    v2 = v2_ref[...]
    lse_all = jnp.zeros((blk, 128), f32)
    for pair in range(heads // 2):
        cols = pl.ds(pair * 128, 128)
        qr = rope(q_ref[:, cols], cosq_ref[...], sinq_ref[...], lane).astype(bf16)
        qr_ref[:, cols] = qr
        outs = []
        for half in range(2):
            mine = (lane < 64) if half == 0 else (lane >= 64)
            qm = jnp.where(mine, qr, jnp.zeros_like(qr))
            score = lax.dot_general(qm, k2, (((1,), (1,)), ((), ())), preferred_element_type=f32)
            score = jnp.where(allowed, score * scale, NEG)
            top = jnp.max(score, axis=1, keepdims=True)
            expo = jnp.where(allowed, jnp.exp(score - top), 0.0)
            total = jnp.sum(expo, axis=1, keepdims=True)
            acc = jnp.dot(expo.astype(bf16), v2, preferred_element_type=f32)
            outs.append(acc / total)
            lse_all = jnp.where(lane == 2 * pair + half, top + jnp.log(total), lse_all)
        o_ref[:, cols] = jnp.where(lane < 64, outs[0], outs[1]).astype(bf16)
    lse_ref[...] = lse_all


def bwd_kernel(heads, qr_ref, k2_ref, v2_ref, o_ref, do_ref, lse_ref, cosq_ref, sinq_ref,
               cosk_ref, sink_ref, qpos_ref, kpos_ref, out_ref, dk_ref, dv_ref):
    scale = 1.0 / math.sqrt(HD)
    blk = qr_ref.shape[0]
    step = pl.program_id(1)

    @pl.when(step == 0)
    def _():
        dk_ref[...] = jnp.zeros_like(dk_ref)
        dv_ref[...] = jnp.zeros_like(dv_ref)

    lane = lax.broadcasted_iota(jnp.int32, (blk, 128), 1)
    allowed = kpos_ref[0] <= qpos_ref[...]
    k2 = k2_ref[...]
    v2 = v2_ref[...]
    rows = pl.ds(pl.multiple_of(step * blk, blk), blk)
    for pair in range(heads // 2):
        cols = pl.ds(pair * 128, 128)
        qr = qr_ref[:, cols]
        do = do_ref[:, cols]
        prod = do.astype(f32) * o_ref[:, cols].astype(f32)
        grads = []
        for half in range(2):
            mine = (lane < 64) if half == 0 else (lane >= 64)
            qm = jnp.where(mine, qr, jnp.zeros_like(qr))
            dm = jnp.where(mine, do, jnp.zeros_like(do))
            delta = jnp.sum(jnp.where(mine, prod, 0.0), axis=1, keepdims=True)
            head = 2 * pair + half
            lse = lse_ref[:, head : head + 1]
            score = lax.dot_general(qm, k2, (((1,), (1,)), ((), ())), preferred_element_type=f32)
            probs = jnp.where(allowed, jnp.exp(score * scale - lse), 0.0)
            dprob = lax.dot_general(dm, v2, (((1,), (1,)), ((), ())), preferred_element_type=f32)
            dscore = (probs * (dprob - delta) * scale).astype(bf16)
            dv_ref[...] += lax.dot_general(
                probs.astype(bf16), dm, (((0,), (0,)), ((), ())), preferred_element_type=f32
            )
            dk_ref[...] += lax.dot_general(
                dscore, qm, (((0,), (0,)), ((), ())), preferred_element_type=f32
            )
            grads.append(jnp.dot(dscore, k2, preferred_element_type=f32))
        dq = jnp.where(lane < 64, grads[0], grads[1])
        out_ref[rows, cols] = rope(dq, cosq_ref[...], -sinq_ref[...], lane).astype(bf16)

    @pl.when(step == pl.num_programs(1) - 1)
    def _():
        dk = dk_ref[...] + pltpu.roll(dk_ref[...], 64, 1)
        dv = dv_ref[...] + pltpu.roll(dv_ref[...], 64, 1)
        klane = lax.broadcasted_iota(jnp.int32, dk.shape, 1)
        rot = rope(dk, cosk_ref[...], -sink_ref[...], klane)
        out_ref[:, heads * 64 :] = jnp.where(klane < 64, rot, dv).astype(bf16)


def attention(qkv, cosine, sine, pos, heads, seqs):
    length = qkv.shape[0] // seqs
    blk = min(256, length)
    nblk = length // blk
    qcols = heads * HD
    row = lambda w: pl.BlockSpec((blk, w), lambda s, i: (s * nblk + i, 0))
    seq = lambda w: pl.BlockSpec((length, w), lambda s, i: (s, 0))
    kv = pl.BlockSpec((length, 128), lambda s, i: (s, qcols // 128))
    qpos = pos.reshape(seqs * length, 1)
    kpos = pos.reshape(seqs, 1, length)
    kpos_spec = pl.BlockSpec((1, 1, length), lambda s, i: (s, 0, 0))
    n = seqs * length
    flops = 4 * n * length * 128 * heads
    fwd = pl.pallas_call(
        functools.partial(fwd_kernel, heads),
        grid=(seqs, nblk),
        in_specs=[row(qcols), kv, row(128), row(128), seq(128), seq(128), row(1), kpos_spec],
        out_specs=[row(qcols), seq(128), seq(128), row(qcols), row(128)],
        out_shape=[
            jax.ShapeDtypeStruct((n, qcols), bf16),
            jax.ShapeDtypeStruct((n, 128), bf16),
            jax.ShapeDtypeStruct((n, 128), bf16),
            jax.ShapeDtypeStruct((n, qcols), bf16),
            jax.ShapeDtypeStruct((n, 128), f32),
        ],
        cost_estimate=pl.CostEstimate(
            flops=flops, bytes_accessed=n * 4096, transcendentals=n * length * heads
        ),
        name="attn_fwd",
    )
    qr, k2, v2, out, lse = fwd(qkv, qkv, cosine, sine, cosine, sine, qpos, kpos)

    def back(d_attn):
        bwd = pl.pallas_call(
            functools.partial(bwd_kernel, heads),
            grid=(seqs, nblk),
            in_specs=[
                row(qcols), seq(128), seq(128), row(qcols), row(qcols), row(128),
                row(128), row(128), seq(128), seq(128), row(1), kpos_spec,
            ],
            out_specs=seq(qcols + 128),
            out_shape=jax.ShapeDtypeStruct((n, qcols + 128), bf16),
            scratch_shapes=[pltpu.VMEM((length, 128), f32), pltpu.VMEM((length, 128), f32)],
            cost_estimate=pl.CostEstimate(
                flops=flops * 5 // 2, bytes_accessed=n * 4096, transcendentals=n * length * heads
            ),
            name="attn_bwd",
        )
        return bwd(qr, k2, v2, out, d_attn, lse, cosine, sine, cosine, sine, qpos, kpos)

    return out, back


def per_device(
    layer_input,
    positions,
    q_weight,
    k_weight,
    v_weight,
    out_weight,
    attn_gain,
    gate_weight,
    up_weight,
    down_weight,
    mlp_gain,
    cotangent,
):
    seqs, tok, width = layer_input.shape
    rows = seqs * tok
    n_f = lax.axis_size("fsdp")
    n_p = lax.axis_size("p")
    n_s = 2 * n_p
    chip = lax.axis_index("p")
    core = lax.axis_index("c")
    own = q_weight.shape[0]
    heads = H // n_s
    qcols = heads * HD
    rep = n_s // KV
    units = gate_weight.shape[1] // (n_f * n_s)
    hid = n_p * units
    fc = ("fsdp", "c")
    pc = ("p", "c")
    a_gain = attn_gain.astype(f32)[:, None]
    m_gain = mlp_gain.astype(f32)[:, None]

    def per_seq(w, width_of):
        return (w.astype(f32) * a_gain).astype(bf16).reshape(own, -1, width_of)

    pack = jnp.concatenate(
        [
            per_seq(q_weight, qcols),
            jnp.repeat(per_seq(k_weight, HD), rep, axis=1),
            jnp.repeat(per_seq(v_weight, HD), rep, axis=1),
        ],
        axis=2,
    )
    pack = lax.all_to_all(pack, pc, split_axis=1, concat_axis=0, tiled=True)
    w_qkv = lax.all_gather(pack.reshape(n_s * own, qcols + 2 * HD), "fsdp", axis=0, tiled=True)
    n_dev = n_f * n_s
    home = [(b, (b % n_f) * n_s + b // n_f) for b in range(n_dev)]
    every = ("fsdp", "p", "c")
    w_out = lax.all_gather(lax.ppermute(out_weight, every, home), "fsdp", axis=0, tiled=True)

    stream = layer_input.astype(f32)
    rinv_one = lax.rsqrt(jnp.mean(stream * stream, axis=-1, keepdims=True) + EPS)
    u_one = plane_gather((stream * rinv_one).astype(bf16))
    length = u_one.shape[1]
    u_one = u_one.reshape(seqs * length, width)
    pos = positions.reshape(seqs, n_p, 2, tok).transpose(0, 2, 1, 3)
    pos = xor_perm(xor_perm(pos, 2, chip), 1, core).reshape(seqs * length)
    lane = jnp.arange(128)
    freq = THETA ** (-((lane % 32).astype(f32) * 2.0 / HD))
    angle = pos.astype(f32)[:, None] * freq[None, :]
    cosine = jnp.cos(angle)
    sine = jnp.where(lane % 64 < 32, -1.0, 1.0) * jnp.sin(angle)
    qkv = jnp.dot(u_one, w_qkv, preferred_element_type=f32)
    attn_out, attn_back = attention(qkv, cosine, sine, pos, heads, seqs)
    part = jnp.dot(attn_out, w_out, preferred_element_type=f32)
    mixed = stream + plane_scatter(part.reshape(seqs, length, width))
    mixed = mixed.reshape(rows, width)
    stream = stream.reshape(rows, width)
    rinv_one = rinv_one.reshape(rows, 1)

    def columns(w):
        w = (w.astype(f32) * m_gain).astype(bf16).reshape(own, n_f, n_p, 2, units)
        return w.transpose(1, 3, 0, 2, 4).reshape(2 * n_f, own, hid)

    gate_up = jnp.concatenate([columns(gate_weight), columns(up_weight)], axis=2)
    gate_up = lax.all_to_all(gate_up, fc, split_axis=0, concat_axis=0, tiled=True)
    gate_up = chip_gather(gate_up.reshape(2 * n_f * own, 2 * hid))
    down = chip_gather_at(down_weight, chip)
    cot = cotangent.reshape(rows, width)
    cot_all = lax.all_gather(cot, fc, axis=0, tiled=True)

    rinv_two = lax.rsqrt(jnp.mean(mixed * mixed, axis=-1, keepdims=True) + EPS)
    u_two = (mixed * rinv_two).astype(bf16).reshape(rows, n_f, n_p, 2 * own)
    u_two = xor_perm(u_two.transpose(0, 2, 1, 3), 1, chip).reshape(rows, width)
    u_two = lax.all_gather(u_two, fc, axis=0, tiled=True)

    pre = jnp.dot(u_two, gate_up, preferred_element_type=f32)
    gate_pre = pre[:, :hid]
    up_pre = pre[:, hid:]
    sigm = jax.nn.sigmoid(gate_pre)
    silu_val = gate_pre * sigm
    hidden = (silu_val * up_pre).astype(bf16)
    mlp_part = jnp.dot(hidden, down, preferred_element_type=f32).astype(bf16)
    d_hidden = jnp.einsum("rd,fd->rf", cot_all, down, preferred_element_type=f32)
    grad_gate = (d_hidden * up_pre * sigm * (1.0 + gate_pre * (1.0 - sigm))).astype(bf16)
    grad_up = (d_hidden * silu_val).astype(bf16)
    grads = jnp.concatenate([grad_gate, grad_up], axis=1)
    d_part = jnp.einsum("rf,df->rd", grads, gate_up, preferred_element_type=f32).astype(bf16)
    z_two = lax.psum_scatter(d_part, fc, scatter_dimension=0, tiled=True)
    z_two = xor_perm(z_two.reshape(rows, n_p, n_f, 2 * own), 1, chip)
    z_two = z_two.transpose(0, 2, 1, 3).reshape(rows, width).astype(f32)
    mlp_own = lax.psum_scatter(mlp_part, fc, scatter_dimension=0, tiled=True)
    output = (mixed + mlp_own.astype(f32)).astype(bf16).reshape(seqs, tok, width)

    d_mixed = (
        cot.astype(f32)
        + rinv_two * z_two
        - mixed * (rinv_two**3) * jnp.mean(z_two * mixed, axis=-1, keepdims=True)
    )
    d_all = plane_gather(d_mixed.astype(bf16).reshape(seqs, tok, width))
    d_all = d_all.reshape(seqs * length, width)

    down_term = jnp.einsum("rf,rd->fd", hidden, cot_all, preferred_element_type=f32).astype(bf16)
    gu_term = jnp.einsum("rd,rf->df", u_two, grads, preferred_element_type=f32).astype(bf16)
    down_share = chip_scatter(down_term, chip)
    gu_sum = chip_scatter(gu_term).astype(bf16).reshape(2 * n_f, own, 2 * hid)
    gu_back = lax.all_to_all(gu_sum, fc, split_axis=0, concat_axis=0, tiled=True)
    gu_back = gu_back.reshape(n_f, 2, own, 2, n_p, units)

    def natural(g):
        return gu_back[:, :, :, g].transpose(2, 0, 3, 1, 4).reshape(own, -1).astype(f32)

    gate_raw = natural(0)
    up_raw = natural(1)
    gate_share = m_gain * gate_raw
    up_share = m_gain * up_raw
    mlp_gain_share = jnp.sum(
        gate_weight.astype(f32) * gate_raw + up_weight.astype(f32) * up_raw, axis=1
    )

    d_attn = jnp.einsum("rd,hd->rh", d_all, w_out, preferred_element_type=f32).astype(bf16)
    d_qkv = attn_back(d_attn)
    z_part = jnp.einsum("rh,dh->rd", d_qkv, w_qkv, preferred_element_type=f32)
    z_one = plane_scatter(z_part.reshape(seqs, length, width)).reshape(rows, width)
    input_grad = (
        d_mixed
        + rinv_one * z_one
        - stream * (rinv_one**3) * jnp.mean(z_one * stream, axis=-1, keepdims=True)
    ).reshape(seqs, tok, width)

    out_term = jnp.einsum("rh,rd->hd", attn_out, d_all, preferred_element_type=f32).astype(bf16)
    out_sum = lax.psum_scatter(out_term, "fsdp", scatter_dimension=0, tiled=True)
    out_share = lax.ppermute(out_sum, every, [(d, b) for b, d in home]).astype(f32)
    qkv_term = jnp.einsum("rd,rh->dh", u_one, d_qkv, preferred_element_type=f32).astype(bf16)
    qkv_sum = lax.psum_scatter(qkv_term, "fsdp", scatter_dimension=0, tiled=True)
    raw = lax.all_to_all(
        qkv_sum.reshape(n_s, own, qcols + 2 * HD), pc, split_axis=0, concat_axis=0, tiled=True
    )
    raw = raw.transpose(1, 0, 2).astype(f32)
    q_raw = raw[:, :, :qcols].reshape(own, H * HD)
    k_raw = raw[:, :, qcols : qcols + HD].reshape(own, KV, rep, HD).sum(2).reshape(own, KV * HD)
    v_raw = raw[:, :, qcols + HD :].reshape(own, KV, rep, HD).sum(2).reshape(own, KV * HD)
    attn_gain_share = (
        jnp.sum(q_weight.astype(f32) * q_raw, axis=1)
        + jnp.sum(k_weight.astype(f32) * k_raw, axis=1)
        + jnp.sum(v_weight.astype(f32) * v_raw, axis=1)
    )
    return (
        output,
        input_grad,
        a_gain * q_raw,
        a_gain * k_raw,
        a_gain * v_raw,
        out_share,
        attn_gain_share,
        gate_share,
        up_share,
        down_share,
        mlp_gain_share,
    )


def solution(mesh):
    n_f = mesh.shape["fsdp"]
    n_s = mesh.shape["seq"]
    fine = Mesh(mesh.devices.reshape(n_f, n_s // 2, 2), ("fsdp", "p", "c"))
    seq = ("p", "c")
    every = ("fsdp", "p", "c")
    act = P("fsdp", seq, None)
    mat = P(every, None)
    vec = P(every)
    in_specs = (act, P("fsdp", None), mat, mat, mat, mat, vec, mat, mat, mat, vec, act)
    out_specs = (act, act, mat, mat, mat, mat, vec, mat, mat, mat, vec)
    return jax.shard_map(
        per_device, mesh=fine, in_specs=in_specs, out_specs=out_specs, check_vma=False
    )
```
